32 devices in a mesh: groups: 2 (over y), dp: 4 (over z), tensor: 4 (over x, core).
Axes of the slice: x: 2, y: 2, z: 4, core: 2. Of those that a mesh axis runs over, the one named last changes fastest.
Arguments:
- tokens: bfloat16 [4096, 4096], P(('groups', 'dp')), parts along dimension 0, may hold values from -6 to 6
- w_query: bfloat16 [4096, 4096], P('dp', 'tensor'), may hold values from -0.09375 to 0.09375
- w_key: bfloat16 [4096, 1024], P('dp', 'tensor'), may hold values from -0.09375 to 0.09375
- w_value: bfloat16 [4096, 1024], P('dp', 'tensor'), may hold values from -0.09375 to 0.09375
- a_query: bfloat16 [8, 4096, 32], P(('groups', 'dp'), 'tensor'), parts along dimension 0, may hold values from -0.09375 to 0.09375
- b_query: bfloat16 [8, 32, 4096], P(('groups', 'dp'), None, 'tensor'), parts along dimension 0, may hold values from -1 to 1
- a_value: bfloat16 [8, 4096, 32], P(('groups', 'dp'), 'tensor'), parts along dimension 0, may hold values from -0.09375 to 0.09375
- b_value: bfloat16 [8, 32, 1024], P(('groups', 'dp'), None, 'tensor'), parts along dimension 0, may hold values from -1 to 1
- adapter_ranks: int32 [8], P('groups'), parts along dimension 0, may hold values from 16 to 32
- adapter_slot: int32 [4], replicated, may hold values from 0 to 3, each once
- block_adapter: int32 [32, 1], P(('groups', 'dp')), parts along dimension 0, may hold values from 0 to 3
- live_tokens: int32 [8], P(('groups', 'dp')), parts along dimension 0, may hold values from 1 to 512, 1280 in all
- d_heads: bfloat16 [4096, 4096], P(('groups', 'dp'), 'tensor'), parts along dimension 0, may hold values from -0.29882812 to 0.29882812
Outputs:
- grad_a_query: float32 [8, 4096, 32], P(('groups', 'dp'), 'tensor'), parts along dimension 0
- grad_b_query: float32 [8, 32, 4096], P(('groups', 'dp'), None, 'tensor'), parts along dimension 0
- grad_a_value: float32 [8, 4096, 32], P(('groups', 'dp'), 'tensor'), parts along dimension 0
- grad_b_value: float32 [8, 32, 1024], P(('groups', 'dp'), None, 'tensor'), parts along dimension 0
The draws below stay inside these ranges and needn't reach their ends.
There are 2 independent parts, one for each index of `groups`. The reference program is written for one: setup_inputs(seed, part) draws one part's arguments, and reference() takes and returns one part's arrays. A program takes and returns all parts, laid end to end along the dimension named above; an argument that names none is the same for every part. Nothing has to cross between parts.
Inputs may be any that keep to these rules, and one draw needn't show every extreme that they name: `adapter_slot`: each slot holds exactly one adapter. `block_adapter`: every adapter is named by some block. `live_tokens`: one index of dp has all its rows live.
All inputs are finite; a program needn't handle non-finite values. No bound on the sum of `live_tokens` on one device may be relied on, other than what follows from the above.
Results may differ from the reference program's by a relative error of at most 0.02.
Values may be sent and summed in bfloat16 or wider, within the bound.
No kernel may reach another device: no remote copies, remote signals or barrier semaphores. Data moves between devices by JAX's collectives and lax.ppermute only.
A program may use at most 64 MiB of HBM per device.

```python
import math
import jax
import jax.numpy as jnp
import numpy as np
from jax import lax

D = 4096
HEADS = 32
KVH = 8
HD = 128
R = 32
REQUEST_ROWS = 128
BLOCKS_DEV = 4
TOK_DEV = 512
TOKENS = 2048
ADAPTERS = 4
N_DP = 4


def touch_ends(result, rng, low, top_value):
    index_at = [jax.random.randint(jax.random.fold_in(rng, axis), (), 0, length) for axis, length in enumerate(result.shape)]
    widest = result.shape.index(max(result.shape))
    next_to = index_at[:widest] + [(index_at[widest] + 1) % result.shape[widest]] + index_at[widest + 1:]
    return result.at[tuple(index_at)].set(low).at[tuple(next_to)].set(top_value)


def block_scale(key, extent, pieces, low, top_value):
    def one(dim, blocks):
        steps = jax.random.uniform(jax.random.fold_in(jax.random.fold_in(key, 6), dim), (blocks,), jnp.float32, low / len(pieces), top_value / len(pieces))
        return jnp.repeat(jnp.exp(steps), extent[dim] // blocks).reshape((-1,) + (1,) * (len(extent) - dim - 1))

    gain = one(*pieces[0])
    for cut in pieces[1:]:
        gain = gain * one(*cut)
    return gain


def distinct(own_key, rows, number_of, top, lift):
    sequence = jax.random.permutation(jax.random.fold_in(own_key, 1), number_of)
    boost = sequence
    for power in range(3):
        boost = boost * boost // number_of
    boost = boost * lift // number_of
    chance = jax.random.randint(jax.random.fold_in(own_key, 2), (rows, number_of), 0, 4096) + boost
    sure = jax.random.permutation(jax.random.fold_in(own_key, 3), rows)[jnp.arange(number_of) % rows]
    chance = jnp.where(jnp.arange(rows)[:, None] == sure[None, :], 1 << 14, chance)
    priority = chance * number_of + jnp.arange(number_of)
    return lax.top_k(priority.astype(jnp.int32), top)[1].astype(jnp.int32)


def split_up(number_of, total, bound, skew):
    portions = [(1 << 20) // math.isqrt(grade ** skew) + 1 for grade in range(2, number_of + 1)]
    surplus, given = total - bound - (number_of - 1), [1] * (number_of - 1)
    while surplus > 0:
        free = [i for i in range(number_of - 1) if given[i] < bound]
        pool, budget = sum([portions[i] for i in free]), surplus
        for i in free:
            more = min(bound - given[i], max(1, budget * portions[i] // pool), surplus)
            given[i] = given[i] + more
            surplus = surplus - more
    return np.array([bound] + given)


def uneven(own_key, number_of, total, bound, skew):
    if number_of == 2:
        one = jax.random.randint(own_key, (), max(1, total - bound), min(bound, total - 1) + 1)
        return jnp.stack([one, total - one])
    lengths = jnp.asarray(split_up(number_of, total, bound, skew), jnp.int32)
    pairs = (number_of - 1) // 2
    source_of, receiver = lengths[1:1 + 2 * pairs:2], lengths[2:2 + 2 * pairs:2]
    slack = jnp.minimum(source_of - 1, bound - receiver)
    passed = jax.random.randint(jax.random.fold_in(own_key, 1), (pairs,), 0, 1 << 20) % (slack + 1)
    lengths = lengths.at[1:1 + 2 * pairs:2].set(source_of - passed).at[2:2 + 2 * pairs:2].set(receiver + passed)
    return lengths[jax.random.permutation(jax.random.fold_in(own_key, 2), number_of)]


def centred(rng, dims, scale, bound, split=(), kind=jnp.bfloat16):
    array = jax.random.normal(rng, dims, jnp.float32) * scale
    if len(split) > 0:
        array = block_scale(rng, dims, split, -0.22, 0.18) * array
    return jnp.clip(array, min=-bound, max=bound).astype(kind)


def setup_inputs(seed: int = 0, part: int = 0) -> dict:
    arg_keys = jax.random.split(jax.random.key(seed), 14)
    part_splits = jax.random.split(jax.random.fold_in(arg_keys[13], part), 14)
    tokens = centred(part_splits[0], (TOKENS, D), 1.0, 6.0, ((0, 4),))
    w_query = centred(arg_keys[1], (D, HEADS * HD), D ** -0.5, 0.09375, ((0, 4), (1, 4)))
    w_key = centred(arg_keys[2], (D, KVH * HD), D ** -0.5, 0.09375, ((0, 4), (1, 4)))
    w_value = centred(arg_keys[3], (D, KVH * HD), D ** -0.5, 0.09375, ((0, 4), (1, 4)))
    a_query = centred(part_splits[4], (ADAPTERS, D, R), D ** -0.5, 0.09375, ((0, 4), (1, 4)))
    b_query = centred(part_splits[5], (ADAPTERS, R, HEADS * HD), R ** -0.5, 1.0, ((0, 4), (2, 4)))
    a_value = centred(part_splits[6], (ADAPTERS, D, R), D ** -0.5, 0.09375, ((0, 4), (1, 4)))
    b_value = centred(part_splits[7], (ADAPTERS, R, KVH * HD), R ** -0.5, 1.0, ((0, 4), (2, 4)))
    adapter_ranks = touch_ends(jax.random.randint(part_splits[8], (ADAPTERS,), R // 2, R + 1), jax.random.fold_in(part_splits[8], 1), R // 2, R).astype(jnp.int32)
    adapter_slot = jax.random.permutation(arg_keys[9], ADAPTERS).astype(jnp.int32)
    block_adapter = distinct(part_splits[10], (TOKENS // REQUEST_ROWS), ADAPTERS, 1, 4096)
    live_tokens = uneven(part_splits[11], N_DP, N_DP * TOK_DEV * 5 // 8, TOK_DEV, 2).astype(jnp.int32)
    d_heads = centred(part_splits[12], (TOKENS, HEADS * HD), 0.05, 0.29882812, ((0, 4), (1, 4)))
    return {"tokens": tokens, "w_query": w_query, "w_key": w_key, "w_value": w_value, "a_query": a_query, "b_query": b_query, "a_value": a_value, "b_value": b_value, "adapter_ranks": adapter_ranks, "adapter_slot": adapter_slot, "block_adapter": block_adapter, "live_tokens": live_tokens, "d_heads": d_heads}


adapter_alpha_factor = 32.0
rope_theta = 500000.0


def rope_tables(length, width):
    halfway = width // 2
    spread = rope_theta ** (-2.0 * jnp.arange(halfway, dtype=jnp.float32) / width)
    angle = jnp.arange(length, dtype=jnp.float32)[:, None] * spread[None, :]
    return jnp.cos(angle), jnp.sin(angle)


def rotate(value_matrix, cosine, sine):
    halfway = value_matrix.shape[-1] // 2
    first = value_matrix[..., :halfway]
    second = value_matrix[..., halfway:]
    cos_grid = cosine[:, None, :]
    sin_grid = sine[:, None, :]
    return jnp.concatenate([first * cos_grid - second * sin_grid, second * cos_grid + first * sin_grid], axis=-1)


def attention_grads(queries, keys, value_matrix, dout, allowed, group):
    request_block_count, length, heads, depth = queries.shape
    kv_heads = keys.shape[2]
    grouped_q = queries.reshape(request_block_count, length, kv_heads, group, depth).astype(jnp.float32)
    grouped_d = dout.reshape(request_block_count, length, kv_heads, group, depth).astype(jnp.float32)
    key_rows = keys.astype(jnp.float32)
    value_rows = value_matrix.astype(jnp.float32)
    scores = jnp.einsum("ntkge,nske->nkgts", grouped_q, key_rows) * (depth ** -0.5)
    scores = jnp.where(allowed[:, None, None], scores, -1e30)
    summit = jnp.max(scores, axis=-1, keepdims=True)
    expo = jnp.exp(scores - summit)
    probs = expo / jnp.sum(expo, axis=-1, keepdims=True)
    dprobs = jnp.einsum("ntkge,nske->nkgts", grouped_d, value_rows)
    dscores = probs * (dprobs - jnp.sum(dprobs * probs, axis=-1, keepdims=True))
    dscore_b = dscores.astype(jnp.bfloat16).astype(jnp.float32)
    dquery = jnp.einsum("nkgts,nske->ntkge", dscore_b, key_rows) * (depth ** -0.5)
    prob_b = probs.astype(jnp.bfloat16).astype(jnp.float32)
    dvalue = jnp.einsum("nkgts,ntkge->nske", prob_b, grouped_d)
    return dquery.reshape(request_block_count, length, heads, depth), dvalue


def reference(tokens, w_query, w_key, w_value, a_query, b_query, a_value, b_value, adapter_ranks, adapter_slot, block_adapter, live_tokens, d_heads):
    cosine, sine = rope_tables(REQUEST_ROWS, HD)
    group = HEADS // KVH
    position = jnp.arange(REQUEST_ROWS, dtype=jnp.int32)
    causal = position[None, :] <= position[:, None]
    diagonal = position[None, :] == position[:, None]
    slot_grid = jnp.arange(ADAPTERS, dtype=jnp.int32)
    rank_grid = jnp.arange(R, dtype=jnp.int32)
    row_index = jnp.arange(TOK_DEV, dtype=jnp.int32).reshape(BLOCKS_DEV, REQUEST_ROWS)

    def device_terms(carry, inputs):
        tok_rows, block_ids, count, dout_rows = inputs
        slot_ids = adapter_slot[block_ids].astype(jnp.int32)
        rank_index_list = adapter_ranks[block_ids]
        adapter_scale = (adapter_alpha_factor / rank_index_list.astype(jnp.float32))[:, None, None]
        keep = (rank_grid[None, :] < rank_index_list[:, None]).astype(jnp.float32)[:, None, :]
        block_tokens = tok_rows.reshape(BLOCKS_DEV, REQUEST_ROWS, D).astype(jnp.float32)
        aq_sel = a_query[slot_ids].astype(jnp.float32)
        av_sel = a_value[slot_ids].astype(jnp.float32)
        selected_query_up = b_query[slot_ids].astype(jnp.float32)
        selected_value_up = b_value[slot_ids].astype(jnp.float32)
        query_down_weight = (jnp.einsum("ntd,ndr->ntr", block_tokens, aq_sel) * keep).astype(jnp.bfloat16).astype(jnp.float32)
        value_down_weight = (jnp.einsum("ntd,ndr->ntr", block_tokens, av_sel) * keep).astype(jnp.bfloat16).astype(jnp.float32)
        frozen_query = jnp.dot(tok_rows, w_query, preferred_element_type=jnp.float32).reshape(BLOCKS_DEV, REQUEST_ROWS, HEADS * HD)
        full_q = frozen_query + adapter_scale * jnp.einsum("zwf,zfy->zwy", query_down_weight, selected_query_up)
        queries = rotate(full_q.reshape(BLOCKS_DEV, REQUEST_ROWS, HEADS, HD), cosine, sine).astype(jnp.bfloat16)
        base_k = jnp.dot(tok_rows, w_key, preferred_element_type=jnp.float32).reshape(BLOCKS_DEV, REQUEST_ROWS, KVH, HD)
        keys = rotate(base_k, cosine, sine).astype(jnp.bfloat16)
        frozen_value = jnp.dot(tok_rows, w_value, preferred_element_type=jnp.float32).reshape(BLOCKS_DEV, REQUEST_ROWS, KVH * HD)
        value_matrix = (frozen_value + adapter_scale * jnp.einsum("zwf,zfy->zwy", value_down_weight, selected_value_up)).astype(jnp.bfloat16)
        value_matrix = value_matrix.reshape(BLOCKS_DEV, REQUEST_ROWS, KVH, HD)
        live = row_index < count
        allowed = causal[None] & (live[:, None, :] | diagonal[None])
        dout = jnp.where(live[:, :, None], dout_rows.reshape(BLOCKS_DEV, REQUEST_ROWS, HEADS * HD), jnp.zeros((), jnp.bfloat16))
        dquery, dvalue = attention_grads(queries, keys, value_matrix, dout.reshape(BLOCKS_DEV, REQUEST_ROWS, HEADS, HD), allowed, group)
        grad_q = rotate(dquery, cosine, -sine).reshape(BLOCKS_DEV, REQUEST_ROWS, HEADS * HD).astype(jnp.bfloat16).astype(jnp.float32)
        grad_v = dvalue.reshape(BLOCKS_DEV, REQUEST_ROWS, KVH * HD).astype(jnp.bfloat16).astype(jnp.float32)
        up_q = adapter_scale * jnp.einsum("ntr,ntc->nrc", query_down_weight, grad_q)
        up_v = adapter_scale * jnp.einsum("ntr,ntc->nrc", value_down_weight, grad_v)
        back_q = (adapter_scale * jnp.einsum("ntc,nrc->ntr", grad_q, selected_query_up) * keep).astype(jnp.bfloat16).astype(jnp.float32)
        back_v = (adapter_scale * jnp.einsum("ntc,nrc->ntr", grad_v, selected_value_up) * keep).astype(jnp.bfloat16).astype(jnp.float32)
        low_q = jnp.einsum("ntd,ntr->ndr", block_tokens, back_q)
        low_v = jnp.einsum("ntd,ntr->ndr", block_tokens, back_v)
        onehot = (slot_grid[:, None] == slot_ids[None, :]).astype(jnp.float32)
        terms = (low_q, up_q, low_v, up_v)
        placed = tuple(jnp.einsum("an,nxy->axy", onehot, item).astype(jnp.bfloat16).astype(jnp.float32) for item in terms)
        return tuple(total + extra for total, extra in zip(carry, placed)), None

    start = (jnp.zeros((ADAPTERS, D, R), jnp.float32), jnp.zeros((ADAPTERS, R, HEADS * HD), jnp.float32),
             jnp.zeros((ADAPTERS, D, R), jnp.float32), jnp.zeros((ADAPTERS, R, KVH * HD), jnp.float32))
    inputs = (tokens.reshape(N_DP, TOK_DEV, D), block_adapter.reshape(N_DP, BLOCKS_DEV), live_tokens,
              d_heads.reshape(N_DP, TOK_DEV, HEADS * HD))
    totals, unused = lax.scan(device_terms, start, inputs)
    return (totals[0], totals[1], totals[2], totals[3])
```

```python
import functools

import jax
import jax.numpy as jnp
from jax import lax
from jax.experimental import pallas as pl
from jax.experimental.pallas import tpu as pltpu
from jax.sharding import PartitionSpec as P

HD = 128
REQUEST_ROWS = 128
LINE_MAX = 8
adapter_alpha_factor = 32.0
rope_theta = 500000.0
F32 = jnp.float32
BF16 = jnp.bfloat16


def rope_tables(length, width):
    halfway = width // 2
    spread = rope_theta ** (-2.0 * jnp.arange(halfway, dtype=F32) / width)
    angle = jnp.arange(length, dtype=F32)[:, None] * spread[None, :]
    cosine, sine = jnp.cos(angle), jnp.sin(angle)
    return (
        jnp.concatenate([cosine, cosine], axis=1),
        jnp.concatenate([-sine, sine], axis=1),
    )


def contract(left, right, dims):
    return lax.dot_general(left, right, (dims, ((), ())), preferred_element_type=F32)


def scalar(ref, kind, block, blocks):
    return ref[2 + kind * blocks + block]


def down_kernel(blocks, rank_width, scalars, tokens, aq, av, out):
    out[0, :rank_width] = contract(aq[0], tokens[...], ((1,), (1,)))
    out[0, rank_width:] = contract(av[0], tokens[...], ((1,), (1,)))


def down_products(scalars, tokens, packs, blocks, width, rank_width):
    return pl.pallas_call(
        functools.partial(down_kernel, blocks, rank_width),
        out_shape=jax.ShapeDtypeStruct((blocks, 2 * rank_width, REQUEST_ROWS), F32),
        grid_spec=pltpu.PrefetchScalarGridSpec(
            num_scalar_prefetch=1,
            grid=(blocks,),
            in_specs=[
                pl.BlockSpec((REQUEST_ROWS, width), lambda n, s: (n, s[1])),
                pl.BlockSpec((1, rank_width, width), lambda n, s: (scalar(s, 0, n, blocks), 0, 0)),
                pl.BlockSpec((1, rank_width, width), lambda n, s: (scalar(s, 0, n, blocks), 0, 1)),
            ],
            out_specs=pl.BlockSpec((1, 2 * rank_width, REQUEST_ROWS), lambda n, s: (n, 0, 0)),
        ),
        name="down",
    )(scalars, tokens, packs, packs)


def attention_kernel(
    blocks, group, rank_width, slots, has_before,
    scalars, acc, down, bq, bv, dout, cosine, sine, *rest,
):
    if has_before:
        before, up_out, back_out, up_sum = rest
    else:
        up_out, back_out, up_sum = rest
    n = pl.program_id(0)
    live = scalars[0]
    rank = scalar(scalars, 1, n, blocks)
    slot = scalar(scalars, 2, n, blocks)
    scale = adapter_alpha_factor / jnp.full((1, 1), rank, jnp.int32).astype(F32)
    wide = group * HD

    @pl.when(n == 0)
    def _():
        up_sum[...] = jnp.zeros_like(up_sum)

    column = lax.broadcasted_iota(jnp.int32, (rank_width, REQUEST_ROWS), 0)
    keep = (column < rank).astype(F32)
    uq = (down[0, :rank_width] * keep).astype(BF16)
    uv = (down[0, rank_width:] * keep).astype(BF16)
    cos, sin = cosine[...], sine[...]

    def rotate(value, sine_part):
        return value * cos + pltpu.roll(value, HD // 2, 1) * sine_part

    query = acc[:, :wide] + scale * contract(uq, bq[0], ((0,), (0,)))
    key = rotate(acc[:, wide : wide + HD], sin).astype(BF16)
    value = (acc[:, wide + HD :] + scale * contract(uv, bv[0], ((0,), (0,)))).astype(BF16)

    position = lax.broadcasted_iota(jnp.int32, (REQUEST_ROWS, REQUEST_ROWS), 0)
    key_position = lax.broadcasted_iota(jnp.int32, (REQUEST_ROWS, REQUEST_ROWS), 1)
    first_row = n * REQUEST_ROWS
    allowed = (key_position <= position) & (
        (key_position + first_row < live) | (key_position == position)
    )
    live_row = position + first_row < live

    grad_value = jnp.zeros((REQUEST_ROWS, HD), F32)
    back_q = jnp.zeros((rank_width, REQUEST_ROWS), F32)
    for h in range(group):
        part = slice(h * HD, (h + 1) * HD)
        head = rotate(query[:, part], sin).astype(BF16)
        grad = jnp.where(live_row, dout[:, part], jnp.zeros((), BF16))
        scores = contract(head, key, ((1,), (1,))) * HD**-0.5
        scores = jnp.where(allowed, scores, -1e30)
        expo = jnp.exp(scores - jnp.max(scores, axis=1, keepdims=True))
        probs = expo / jnp.sum(expo, axis=1, keepdims=True)
        dprobs = contract(grad, value, ((1,), (1,)))
        dscores = probs * (dprobs - jnp.sum(dprobs * probs, axis=1, keepdims=True))
        dquery = contract(dscores.astype(BF16), key, ((1,), (0,))) * HD**-0.5
        grad_query = rotate(dquery, -sin).astype(BF16)
        grad_value += contract(probs.astype(BF16), grad, ((0,), (0,)))
        up_sum[slot, :, part] += scale * contract(uq, grad_query, ((1,), (0,)))
        back_q += contract(bq[0, :, part], grad_query, ((1,), (1,)))
    grad_value = grad_value.astype(BF16)
    up_sum[slot, :, wide:] += scale * contract(uv, grad_value, ((1,), (0,)))
    back_v = contract(bv[0], grad_value, ((1,), (1,)))
    if has_before:
        back_out[0, :rank_width] = before[0, :rank_width] + scale * back_q
        back_out[0, rank_width:] = before[0, rank_width:] + scale * back_v
    else:
        back_out[0, :rank_width] = scale * back_q
        back_out[0, rank_width:] = scale * back_v

    @pl.when(n == blocks - 1)
    def _():
        up_out[...] = up_sum[...].astype(BF16)


def attention(scalars, acc, down, packs, dout, tables, before, j, blocks, group, width, slots):
    rank_width = down.shape[1] // 2
    wide = group * HD
    query_columns = dout.shape[1]
    query_at = 2 * width // wide + j
    value_at = (2 * width + query_columns) // HD + j
    back_spec = pl.BlockSpec((1, 2 * rank_width, REQUEST_ROWS), lambda n, s: (n, 0, 0))
    table_spec = pl.BlockSpec((REQUEST_ROWS, HD), lambda n, s: (0, 0))
    in_specs = [
        pl.BlockSpec((REQUEST_ROWS, wide + 2 * HD), lambda n, s: (n, 0)),
        back_spec,
        pl.BlockSpec((1, rank_width, wide), lambda n, s: (scalar(s, 0, n, blocks), 0, query_at)),
        pl.BlockSpec((1, rank_width, HD), lambda n, s: (scalar(s, 0, n, blocks), 0, value_at)),
        pl.BlockSpec((REQUEST_ROWS, wide), lambda n, s: (n, j)),
        table_spec,
        table_spec,
    ]
    operands = [acc, down, packs, packs, dout, *tables]
    if before is not None:
        in_specs.append(back_spec)
        operands.append(before)
    return pl.pallas_call(
        functools.partial(attention_kernel, blocks, group, rank_width, slots, before is not None),
        out_shape=(
            jax.ShapeDtypeStruct((slots, rank_width, wide + HD), BF16),
            jax.ShapeDtypeStruct((blocks, 2 * rank_width, REQUEST_ROWS), F32),
        ),
        grid_spec=pltpu.PrefetchScalarGridSpec(
            num_scalar_prefetch=1,
            grid=(blocks,),
            in_specs=in_specs,
            out_specs=(
                pl.BlockSpec((slots, rank_width, wide + HD), lambda n, s: (0, 0, 0)),
                back_spec,
            ),
            scratch_shapes=[pltpu.VMEM((slots, rank_width, wide + HD), F32)],
        ),
        name="attention",
    )(scalars, *operands)


def low_kernel(blocks, rank_width, scalars, tokens, back, out, total):
    n = pl.program_id(0)
    rank = scalar(scalars, 1, n, blocks)
    slot = scalar(scalars, 2, n, blocks)

    @pl.when(n == 0)
    def _():
        total[...] = jnp.zeros_like(total)

    row = lax.broadcasted_iota(jnp.int32, (2 * rank_width, REQUEST_ROWS), 0)
    row = jnp.where(row >= rank_width, row - rank_width, row)
    kept = (back[0] * (row < rank).astype(F32)).astype(BF16)
    total[slot] += contract(kept, tokens[...], ((1,), (0,)))

    @pl.when(n == blocks - 1)
    def _():
        out[...] = total[...].astype(BF16)


def low_products(scalars, tokens, back, blocks, width, slots):
    rank_width = back.shape[1] // 2
    return pl.pallas_call(
        functools.partial(low_kernel, blocks, rank_width),
        out_shape=jax.ShapeDtypeStruct((slots, 2 * rank_width, width), BF16),
        grid_spec=pltpu.PrefetchScalarGridSpec(
            num_scalar_prefetch=1,
            grid=(blocks,),
            in_specs=[
                pl.BlockSpec((REQUEST_ROWS, width), lambda n, s: (n, s[1])),
                pl.BlockSpec((1, 2 * rank_width, REQUEST_ROWS), lambda n, s: (n, 0, 0)),
            ],
            out_specs=pl.BlockSpec((slots, 2 * rank_width, width), lambda n, s: (0, 0, 0)),
            scratch_shapes=[pltpu.VMEM((slots, 2 * rank_width, width), F32)],
        ),
        name="low",
    )(scalars, tokens, back)


def sum_over(value, axis, send_type):
    count = lax.axis_size(axis)
    step = 1
    while step < count:
        other = lax.ppermute(value.astype(send_type), axis, [(i, i ^ step) for i in range(count)])
        value = value + other.astype(value.dtype)
        step *= 2
    return value


def along_line(piece, count):
    left, right, found = piece, piece, []
    for t in range(count - 1):
        left = lax.ppermute(left, "dp", [(i, i + 1) for i in range(t, count - 1)])
        right = lax.ppermute(right, "dp", [(i, i - 1) for i in range(1, count - t)])
        found.append((t, left, right))
    return found


def line_blocks(piece, count):
    me = lax.axis_index("dp")
    blocks = []
    for t, left, right in along_line(piece, count):
        lefts = [i for i in range(count) if i > t]
        rights = [i for i in range(count) if i + t + 1 < count]
        if set(lefts) & set(rights):
            blocks.append((me - 1 - t, left, lefts))
            blocks.append((me + 1 + t, right, rights))
        else:
            owner = jnp.where(me > t, me - 1 - t, me + 1 + t)
            blocks.append((owner, jnp.where(me > t, left, right), lefts + rights))
    return blocks


def swap_groups(piece, holders, groups, count):
    pairs = [
        (g * count + d, ((g + 1) % groups) * count + d) for g in range(groups) for d in holders
    ]
    return lax.ppermute(piece, ("groups", "dp"), pairs)


def on_device(
    tokens, w_query, w_key, w_value, a_query, b_query, a_value, b_value,
    adapter_ranks, adapter_slot, block_adapter, live_tokens, d_heads,
):
    blocks = tokens.shape[0] // REQUEST_ROWS
    owned, width, rank_width = a_query.shape
    shard_rows, query_columns = w_query.shape
    value_columns = w_key.shape[1]
    local_kv = value_columns // HD
    group = query_columns // value_columns
    wide = group * HD
    count, groups = lax.axis_size("dp"), lax.axis_size("groups")
    slots = owned * count
    me, my_group = lax.axis_index("dp"), lax.axis_index("groups")
    by_line = count <= LINE_MAX and groups == 2 and owned == 1 and count % 2 == 0

    block_ids = block_adapter[:, 0]
    slot_ids = adapter_slot[block_ids]
    ranks = adapter_ranks[block_ids]
    pack = jnp.concatenate(
        [jnp.swapaxes(a_query, 1, 2), jnp.swapaxes(a_value, 1, 2), b_query, b_value], axis=2
    )
    pieces = [
        jnp.concatenate(
            [
                w_query[:, j * wide : (j + 1) * wide],
                w_key[:, j * HD : (j + 1) * HD],
                w_value[:, j * HD : (j + 1) * HD],
            ],
            axis=1,
        )
        for j in range(local_kv)
    ]

    if by_line:
        half = shard_rows // groups
        sums = []
        found_packs = None
        for piece in pieces:
            mine = lax.dynamic_slice_in_dim(piece, my_group * half, half, 0)
            arrivals = line_blocks(mine, count)
            if found_packs is None:
                found_packs = line_blocks(pack, count)
            total = jnp.dot(
                lax.dynamic_slice_in_dim(tokens, me * shard_rows, shard_rows, 1),
                piece,
                preferred_element_type=F32,
            )
            for owner, block, holders in arrivals:
                other = swap_groups(block, holders, groups, count)
                for rows, which in ((block, my_group), (other, 1 - my_group)):
                    start = owner * shard_rows + which * half
                    total = total + jnp.dot(
                        lax.dynamic_slice_in_dim(tokens, start, half, 1),
                        rows,
                        preferred_element_type=F32,
                    )
            sums.append(total)
        packs = jnp.concatenate([pack] + [block for _, block, _ in found_packs], axis=0)
        place = jnp.zeros_like(slot_ids)
        for k, (owner, _, holders) in enumerate(found_packs):
            place = jnp.where(slot_ids == owner, k + 1, place)
    else:
        packs = lax.all_gather(pack, "dp", axis=0, tiled=True)
        place = slot_ids
        sums = [
            jnp.dot(
                tokens,
                lax.all_gather(piece, "dp", axis=0, tiled=True),
                preferred_element_type=F32,
            )
            for piece in pieces
        ]

    scalars = jnp.concatenate(
        [
            live_tokens[:1],
            lax.axis_index("tensor").astype(jnp.int32)[None],
            place.astype(jnp.int32),
            ranks,
            slot_ids,
        ]
    )
    down = down_products(scalars, tokens, packs, blocks, width, rank_width)
    down = sum_over(down, "tensor", F32)
    tables = rope_tables(REQUEST_ROWS, HD)
    ups, back = [], None
    for j in range(local_kv):
        up, back = attention(
            scalars, sums[j], down, packs, d_heads, tables, back, j, blocks, group, width, slots
        )
        ups.append(up)
    ups = [lax.all_to_all(up, "dp", split_axis=0, concat_axis=0, tiled=True) for up in ups]
    back = sum_over(back, "tensor", F32)
    low = low_products(scalars, tokens, back, blocks, width, slots)
    low = lax.all_to_all(low, "dp", split_axis=0, concat_axis=0, tiled=True)

    def summed(item):
        item = item.astype(F32).reshape((count, owned) + item.shape[1:])
        return jnp.sum(item, axis=0)

    low = summed(low)
    ups = [summed(up) for up in ups]
    return (
        jnp.swapaxes(low[:, :rank_width], 1, 2),
        jnp.concatenate([up[:, :, :wide] for up in ups], axis=2),
        jnp.swapaxes(low[:, rank_width:], 1, 2),
        jnp.concatenate([up[:, :, wide:] for up in ups], axis=2),
    )


def solution(mesh):
    in_specs = (
        P(("groups", "dp"), None),
        P("dp", "tensor"),
        P("dp", "tensor"),
        P("dp", "tensor"),
        P(("groups", "dp"), "tensor", None),
        P(("groups", "dp"), None, "tensor"),
        P(("groups", "dp"), "tensor", None),
        P(("groups", "dp"), None, "tensor"),
        P("groups"),
        P(),
        P(("groups", "dp"), None),
        P(("groups", "dp")),
        P(("groups", "dp"), "tensor"),
    )
    out_specs = (
        P(("groups", "dp"), "tensor", None),
        P(("groups", "dp"), None, "tensor"),
        P(("groups", "dp"), "tensor", None),
        P(("groups", "dp"), None, "tensor"),
    )
    return jax.shard_map(
        on_device, mesh=mesh, in_specs=in_specs, out_specs=out_specs, check_vma=False
    )
```

```python
import functools

import jax
import jax.numpy as jnp
from jax import lax
from jax.experimental import pallas as pl
from jax.experimental.pallas import tpu as pltpu
from jax.sharding import PartitionSpec as P

HD = 128
REQUEST_ROWS = 128
LINE_MAX = 8
adapter_alpha_factor = 32.0
rope_theta = 500000.0
F32 = jnp.float32
BF16 = jnp.bfloat16


def rope_tables(length, width):
    halfway = width // 2
    spread = rope_theta ** (-2.0 * jnp.arange(halfway, dtype=F32) / width)
    angle = jnp.arange(length, dtype=F32)[:, None] * spread[None, :]
    cosine, sine = jnp.cos(angle), jnp.sin(angle)
    cosine = jnp.concatenate([cosine, cosine], axis=1)
    sine = jnp.concatenate([-sine, sine], axis=1)
    return cosine, sine, cosine.T, -sine.T


def contract(left, right, dims):
    return lax.dot_general(left, right, (dims, ((), ())), preferred_element_type=F32)


def scalar(ref, kind, block, blocks):
    return ref[2 + kind * blocks + block]


def block_rows(n):
    return slice(n * REQUEST_ROWS, (n + 1) * REQUEST_ROWS)


def down_kernel(blocks, rank_width, width, scalars, tokens, packs, out):
    for n in range(blocks):
        place = scalar(scalars, 0, n, blocks)
        rows = tokens[block_rows(n)]
        for k in range(2):
            factor = packs[place, :, k * width : (k + 1) * width]
            out[n, k * rank_width : (k + 1) * rank_width] = contract(factor, rows, ((1,), (1,)))


def whole(shape):
    return pl.BlockSpec(shape, lambda i, s: (0,) * len(shape))


def down_products(scalars, tokens, packs, blocks, width):
    rank_width = packs.shape[1]
    return pl.pallas_call(
        functools.partial(down_kernel, blocks, rank_width, width),
        out_shape=jax.ShapeDtypeStruct((blocks, 2 * rank_width, REQUEST_ROWS), F32),
        grid_spec=pltpu.PrefetchScalarGridSpec(
            num_scalar_prefetch=1,
            grid=(1,),
            in_specs=[
                pl.BlockSpec((tokens.shape[0], width), lambda i, s: (0, s[1])),
                pl.BlockSpec((packs.shape[0], rank_width, 2 * width), lambda i, s: (0, 0, 0)),
            ],
            out_specs=whole((blocks, 2 * rank_width, REQUEST_ROWS)),
        ),
        name="down",
    )(scalars, tokens, packs)


def attention_kernel(
    blocks, group, rank_width, value_at,
    scalars, acc, down, down_other, factors, dout, cosine, sine, cosine_t, sine_t, before,
    up_out, back_out, up_sum,
):
    live = scalars[0]
    wide = group * HD
    half = HD // 2
    shape = (REQUEST_ROWS, REQUEST_ROWS)
    cos, sin, cos_t, sin_t = cosine[...], sine[...], cosine_t[...], sine_t[...]
    key_at = lax.broadcasted_iota(jnp.int32, shape, 0)
    query_at = lax.broadcasted_iota(jnp.int32, shape, 1)
    column = lax.broadcasted_iota(jnp.int32, (2 * rank_width, REQUEST_ROWS), 0)
    column = jnp.where(column >= rank_width, column - rank_width, column)
    up_sum[...] = jnp.zeros_like(up_sum)

    def rotate(value):
        return value * cos + pltpu.roll(value, half, 1) * sin

    def stack(value):
        return jnp.concatenate([value[:, h * HD : (h + 1) * HD] for h in range(group)], axis=0)

    states = []
    for n in range(blocks):
        rows = block_rows(n)
        place = scalar(scalars, 0, n, blocks)
        rank = scalar(scalars, 1, n, blocks)
        scale = adapter_alpha_factor / jnp.full((1, 1), rank, jnp.int32).astype(F32)
        u = ((down[n] + down_other[n]) * (column < rank).astype(F32)).astype(BF16)
        uq, uv = u[:rank_width], u[rank_width:]
        bq, bv = factors[place, :, :wide], factors[place, :, value_at : value_at + HD]
        query = acc[rows, :wide] + scale * contract(uq, bq, ((0,), (0,)))
        value = acc[rows, wide + HD :] + scale * contract(uv, bv, ((0,), (0,)))
        query = jnp.concatenate(
            [rotate(query[:, h * HD : (h + 1) * HD]).astype(BF16) for h in range(group)], axis=0
        )
        key = rotate(acc[rows, wide : wide + HD]).astype(BF16)
        live_row = lax.broadcasted_iota(jnp.int32, (REQUEST_ROWS, wide), 0) + n * REQUEST_ROWS < live
        grad = stack(jnp.where(live_row, dout[rows], jnp.zeros((), BF16)))
        states.append((n, rank, scale, uq, uv, bq, bv, query, key, value.astype(BF16), grad))

    for n, rank, scale, uq, uv, bq, bv, query, key, value, grad in states:
        slot = scalar(scalars, 2, n, blocks)
        allowed = (key_at <= query_at) & ((key_at + n * REQUEST_ROWS < live) | (key_at == query_at))
        allowed = jnp.concatenate([allowed.astype(F32)] * group, axis=1) > 0.5
        scores = contract(key, query, ((1,), (1,))) * HD**-0.5
        dprobs = contract(value, grad, ((1,), (1,)))
        scores = jnp.where(allowed, scores, -1e30)
        expo = jnp.exp(scores - jnp.max(scores, axis=0, keepdims=True))
        probs = expo * (1.0 / jnp.sum(expo, axis=0, keepdims=True))
        dscores = probs * (dprobs - jnp.sum(dprobs * probs, axis=0, keepdims=True))
        dquery = contract(key, dscores.astype(BF16), ((0,), (0,))) * HD**-0.5
        grad_value = contract(probs.astype(BF16), grad, ((1,), (0,))).astype(BF16)
        turned = jnp.concatenate([dquery[half:], dquery[:half]], axis=0)
        back_q = jnp.zeros((rank_width, REQUEST_ROWS), F32)
        for h in range(group):
            part = slice(h * HD, (h + 1) * HD)
            grad_query = (dquery[:, part] * cos_t + turned[:, part] * sin_t).astype(BF16)
            up_sum[slot, :, part] += scale * contract(uq, grad_query, ((1,), (1,)))
            back_q += contract(bq[:, part], grad_query, ((1,), (0,)))
        up_sum[slot, :, wide:] += scale * contract(uv, grad_value, ((1,), (0,)))
        back_v = contract(bv, grad_value, ((1,), (1,)))
        back_out[n, :rank_width] = before[n, :rank_width] + scale * back_q
        back_out[n, rank_width:] = before[n, rank_width:] + scale * back_v
    up_out[...] = up_sum[...].astype(BF16)


def attention(scalars, acc, downs, packs, dout, tables, before, j, blocks, group, width, slots):
    rank_width = packs.shape[1]
    wide = group * HD
    query_columns = dout.shape[1]
    factors = packs[:, :, 2 * width + j * wide : 2 * width + (j + 1) * wide]
    value_at = 2 * width + query_columns + j * HD
    factors = jnp.concatenate([factors, packs[:, :, value_at : value_at + HD]], axis=2)
    small = (blocks, 2 * rank_width, REQUEST_ROWS)
    up_shape = (slots, rank_width, wide + HD)
    return pl.pallas_call(
        functools.partial(attention_kernel, blocks, group, rank_width, wide),
        out_shape=(jax.ShapeDtypeStruct(up_shape, BF16), jax.ShapeDtypeStruct(small, F32)),
        grid_spec=pltpu.PrefetchScalarGridSpec(
            num_scalar_prefetch=1,
            grid=(1,),
            in_specs=[
                whole(acc.shape),
                whole(small),
                whole(small),
                whole(factors.shape),
                pl.BlockSpec((dout.shape[0], wide), lambda i, s: (0, j)),
                *[whole(table.shape) for table in tables],
                whole(small),
            ],
            out_specs=(whole(up_shape), whole(small)),
            scratch_shapes=[pltpu.VMEM(up_shape, F32)],
        ),
        name="attention",
    )(scalars, acc, *downs, factors, dout, *tables, before)


def low_kernel(blocks, rank_width, scalars, tokens, back, back_other, out, total):
    total[...] = jnp.zeros_like(total)
    row = lax.broadcasted_iota(jnp.int32, (2 * rank_width, REQUEST_ROWS), 0)
    row = jnp.where(row >= rank_width, row - rank_width, row)
    for n in range(blocks):
        rank = scalar(scalars, 1, n, blocks)
        slot = scalar(scalars, 2, n, blocks)
        kept = ((back[n] + back_other[n]) * (row < rank).astype(F32)).astype(BF16)
        total[slot] += contract(kept, tokens[block_rows(n)], ((1,), (0,)))
    out[...] = total[...].astype(BF16)


def low_products(scalars, tokens, backs, blocks, width, slots):
    small = backs[0].shape
    rank_width = small[1] // 2
    out = (slots, 2 * rank_width, width)
    return pl.pallas_call(
        functools.partial(low_kernel, blocks, rank_width),
        out_shape=jax.ShapeDtypeStruct(out, BF16),
        grid_spec=pltpu.PrefetchScalarGridSpec(
            num_scalar_prefetch=1,
            grid=(1,),
            in_specs=[
                pl.BlockSpec((tokens.shape[0], width), lambda i, s: (0, s[1])),
                whole(small),
                whole(small),
            ],
            out_specs=whole(out),
            scratch_shapes=[pltpu.VMEM(out, F32)],
        ),
        name="low",
    )(scalars, tokens, *backs)


def halves_over(value, axis):
    count = lax.axis_size(axis)
    step = 1
    pair = (value, jnp.zeros_like(value))
    while step < count:
        value = value if step == 1 else pair[0] + pair[1]
        pair = (value, lax.ppermute(value, axis, [(i, i ^ step) for i in range(count)]))
        step *= 2
    return pair


def along_line(piece, count):
    left, right, found = piece, piece, []
    for t in range(count - 1):
        left = lax.ppermute(left, "dp", [(i, i + 1) for i in range(t, count - 1)])
        right = lax.ppermute(right, "dp", [(i, i - 1) for i in range(1, count - t)])
        found.append((t, left, right))
    return found


def line_blocks(piece, count):
    me = lax.axis_index("dp")
    blocks = []
    for t, left, right in along_line(piece, count):
        lefts = [i for i in range(count) if i > t]
        rights = [i for i in range(count) if i + t + 1 < count]
        if set(lefts) & set(rights):
            blocks.append((me - 1 - t, left, lefts))
            blocks.append((me + 1 + t, right, rights))
        else:
            owner = jnp.where(me > t, me - 1 - t, me + 1 + t)
            blocks.append((owner, jnp.where(me > t, left, right), lefts + rights))
    return blocks


def swap_groups(piece, holders, groups, count):
    pairs = [
        (g * count + d, ((g + 1) % groups) * count + d) for g in range(groups) for d in holders
    ]
    return lax.ppermute(piece, ("groups", "dp"), pairs)


def on_device(
    tokens, w_query, w_key, w_value, a_query, b_query, a_value, b_value,
    adapter_ranks, adapter_slot, block_adapter, live_tokens, d_heads,
):
    blocks = tokens.shape[0] // REQUEST_ROWS
    owned, width, rank_width = a_query.shape
    shard_rows, query_columns = w_query.shape
    value_columns = w_key.shape[1]
    local_kv = value_columns // HD
    group = query_columns // value_columns
    wide = group * HD
    count, groups = lax.axis_size("dp"), lax.axis_size("groups")
    slots = owned * count
    me, my_group = lax.axis_index("dp"), lax.axis_index("groups")
    by_line = count <= LINE_MAX and groups == 2 and owned == 1 and count % 2 == 0

    block_ids = block_adapter[:, 0]
    slot_ids = adapter_slot[block_ids]
    ranks = adapter_ranks[block_ids]
    pack = jnp.concatenate(
        [jnp.swapaxes(a_query, 1, 2), jnp.swapaxes(a_value, 1, 2), b_query, b_value], axis=2
    )
    pieces = [
        jnp.concatenate(
            [
                w_query[:, j * wide : (j + 1) * wide],
                w_key[:, j * HD : (j + 1) * HD],
                w_value[:, j * HD : (j + 1) * HD],
            ],
            axis=1,
        )
        for j in range(local_kv)
    ]

    if by_line:
        half = shard_rows // groups
        sums = []
        found_packs = None
        for piece in pieces:
            mine = lax.dynamic_slice_in_dim(piece, my_group * half, half, 0)
            arrivals = line_blocks(mine, count)
            if found_packs is None:
                found_packs = line_blocks(pack, count)
            total = jnp.dot(
                lax.dynamic_slice_in_dim(tokens, me * shard_rows, shard_rows, 1),
                piece,
                preferred_element_type=F32,
            )
            for owner, block, holders in arrivals:
                other = swap_groups(block, holders, groups, count)
                for rows, which in ((block, my_group), (other, 1 - my_group)):
                    start = owner * shard_rows + which * half
                    total = total + jnp.dot(
                        lax.dynamic_slice_in_dim(tokens, start, half, 1),
                        rows,
                        preferred_element_type=F32,
                    )
            sums.append(total)
        packs = jnp.concatenate([pack] + [block for _, block, _ in found_packs], axis=0)
        place = jnp.zeros_like(slot_ids)
        for k, (owner, _, holders) in enumerate(found_packs):
            place = jnp.where(slot_ids == owner, k + 1, place)
    else:
        packs = lax.all_gather(pack, "dp", axis=0, tiled=True)
        place = slot_ids
        sums = [
            jnp.dot(
                tokens,
                lax.all_gather(piece, "dp", axis=0, tiled=True),
                preferred_element_type=F32,
            )
            for piece in pieces
        ]

    scalars = jnp.concatenate(
        [
            live_tokens[:1],
            lax.axis_index("tensor").astype(jnp.int32)[None],
            place.astype(jnp.int32),
            ranks,
            slot_ids,
        ]
    )
    down = down_products(scalars, tokens, packs, blocks, width)
    downs = halves_over(down, "tensor")
    tables = rope_tables(REQUEST_ROWS, HD)
    ups, back = [], jnp.zeros_like(down)
    for j in range(local_kv):
        up, back = attention(
            scalars, sums[j], downs, packs, d_heads, tables, back, j, blocks, group, width, slots
        )
        ups.append(up)
    ups = [lax.all_to_all(up, "dp", split_axis=0, concat_axis=0, tiled=True) for up in ups]
    low = low_products(scalars, tokens, halves_over(back, "tensor"), blocks, width, slots)
    low = lax.all_to_all(low, "dp", split_axis=0, concat_axis=0, tiled=True)

    def summed(item):
        item = item.astype(F32).reshape((count, owned) + item.shape[1:])
        return jnp.sum(item, axis=0)

    low = summed(low)
    ups = [summed(up) for up in ups]
    return (
        jnp.swapaxes(low[:, :rank_width], 1, 2),
        jnp.concatenate([up[:, :, :wide] for up in ups], axis=2),
        jnp.swapaxes(low[:, rank_width:], 1, 2),
        jnp.concatenate([up[:, :, wide:] for up in ups], axis=2),
    )


def solution(mesh):
    in_specs = (
        P(("groups", "dp"), None),
        P("dp", "tensor"),
        P("dp", "tensor"),
        P("dp", "tensor"),
        P(("groups", "dp"), "tensor", None),
        P(("groups", "dp"), None, "tensor"),
        P(("groups", "dp"), "tensor", None),
        P(("groups", "dp"), None, "tensor"),
        P("groups"),
        P(),
        P(("groups", "dp"), None),
        P(("groups", "dp")),
        P(("groups", "dp"), "tensor"),
    )
    out_specs = (
        P(("groups", "dp"), "tensor", None),
        P(("groups", "dp"), None, "tensor"),
        P(("groups", "dp"), "tensor", None),
        P(("groups", "dp"), None, "tensor"),
    )
    return jax.shard_map(
        on_device, mesh=mesh, in_specs=in_specs, out_specs=out_specs, check_vma=False
    )
```

```python
import functools

import jax
import jax.numpy as jnp
from jax import lax
from jax.experimental import pallas as pl
from jax.experimental.pallas import tpu as pltpu
from jax.sharding import PartitionSpec as P


HD = 128
REQUEST_ROWS = 128
adapter_alpha_factor = 32.0
rope_theta = 500000.0
F32 = jnp.float32
BF16 = jnp.bfloat16


def rope_tables(length, width):
    halfway = width // 2
    spread = rope_theta ** (-2.0 * jnp.arange(halfway, dtype=F32) / width)
    angle = jnp.arange(length, dtype=F32)[:, None] * spread[None, :]
    cosine, sine = jnp.cos(angle), jnp.sin(angle)
    cosine = jnp.concatenate([cosine, cosine], axis=1)
    sine = jnp.concatenate([-sine, sine], axis=1)
    return cosine, sine, cosine.T, -sine.T


def contract(left, right, dims):
    return lax.dot_general(left, right, (dims, ((), ())), preferred_element_type=F32)


def scalar(ref, kind, block, blocks):
    return ref[2 + kind * blocks + block]


def block_rows(n):
    return slice(n * REQUEST_ROWS, (n + 1) * REQUEST_ROWS)


def down_kernel(blocks, rank_width, width, scalars, tokens, packs, out):
    for n in range(blocks):
        place = scalar(scalars, 0, n, blocks)
        rows = tokens[block_rows(n)]
        for k in range(2):
            factor = packs[place, :, k * width : (k + 1) * width]
            out[n, k * rank_width : (k + 1) * rank_width] = contract(factor, rows, ((1,), (1,)))


def whole(shape):
    return pl.BlockSpec(shape, lambda i, s: (0,) * len(shape))


def down_products(scalars, tokens, packs, blocks, width):
    rank_width = packs.shape[1]
    return pl.pallas_call(
        functools.partial(down_kernel, blocks, rank_width, width),
        out_shape=jax.ShapeDtypeStruct((blocks, 2 * rank_width, REQUEST_ROWS), F32),
        grid_spec=pltpu.PrefetchScalarGridSpec(
            num_scalar_prefetch=1,
            grid=(1,),
            in_specs=[
                pl.BlockSpec((tokens.shape[0], width), lambda i, s: (0, s[1])),
                pl.BlockSpec((packs.shape[0], rank_width, 2 * width), lambda i, s: (0, 0, 0)),
            ],
            out_specs=whole((blocks, 2 * rank_width, REQUEST_ROWS)),
        ),
        name="down",
    )(scalars, tokens, packs)


def attention_kernel(
    blocks, group, rank_width, query_from, value_from, has_before,
    scalars, acc, down, down_other, packs, dout, cosine, sine, cosine_t, sine_t, *rest,
):
    before = rest[0] if has_before else None
    up_out, back_out, up_sum = rest[-3:]
    live = scalars[0]
    wide = group * HD
    half = HD // 2
    shape = (REQUEST_ROWS, REQUEST_ROWS)
    cos, sin, cos_t, sin_t = cosine[...], sine[...], cosine_t[...], sine_t[...]
    key_at = lax.broadcasted_iota(jnp.int32, shape, 0)
    query_at = lax.broadcasted_iota(jnp.int32, shape, 1)
    column = lax.broadcasted_iota(jnp.int32, (2 * rank_width, REQUEST_ROWS), 0)
    column = jnp.where(column >= rank_width, column - rank_width, column)
    up_sum[...] = jnp.zeros_like(up_sum)

    def rotate(value):
        return value * cos + pltpu.roll(value, half, 1) * sin

    def stack(value):
        return jnp.concatenate([value[:, h * HD : (h + 1) * HD] for h in range(group)], axis=0)

    states = []
    for n in range(blocks):
        rows = block_rows(n)
        place = scalar(scalars, 0, n, blocks)
        rank = scalar(scalars, 1, n, blocks)
        scale = adapter_alpha_factor / jnp.full((1, 1), rank, jnp.int32).astype(F32)
        u = ((down[n] + down_other[n]) * (column < rank).astype(F32)).astype(BF16)
        uq, uv = u[:rank_width], u[rank_width:]
        bq = packs[place, :, query_from : query_from + wide]
        bv = packs[place, :, value_from : value_from + HD]
        query = acc[rows, :wide] + scale * contract(uq, bq, ((0,), (0,)))
        value = acc[rows, wide + HD :] + scale * contract(uv, bv, ((0,), (0,)))
        query = jnp.concatenate(
            [rotate(query[:, h * HD : (h + 1) * HD]).astype(BF16) for h in range(group)], axis=0
        )
        key = rotate(acc[rows, wide : wide + HD]).astype(BF16)
        live_row = lax.broadcasted_iota(jnp.int32, (REQUEST_ROWS, wide), 0) + n * REQUEST_ROWS < live
        grad = stack(jnp.where(live_row, dout[rows], jnp.zeros((), BF16)))
        states.append((n, rank, scale, uq, uv, bq, bv, query, key, value.astype(BF16), grad))

    for n, rank, scale, uq, uv, bq, bv, query, key, value, grad in states:
        slot = scalar(scalars, 2, n, blocks)
        allowed = (key_at <= query_at) & ((key_at + n * REQUEST_ROWS < live) | (key_at == query_at))
        allowed = jnp.concatenate([allowed.astype(F32)] * group, axis=1) > 0.5
        scores = contract(key, query, ((1,), (1,))) * HD**-0.5
        dprobs = contract(value, grad, ((1,), (1,)))
        scores = jnp.where(allowed, scores, -1e30)
        expo = jnp.exp(scores - jnp.max(scores, axis=0, keepdims=True))
        probs = expo * (1.0 / jnp.sum(expo, axis=0, keepdims=True))
        dscores = probs * (dprobs - jnp.sum(dprobs * probs, axis=0, keepdims=True))
        dquery = contract(key, dscores.astype(BF16), ((0,), (0,))) * HD**-0.5
        grad_value = contract(probs.astype(BF16), grad, ((1,), (0,))).astype(BF16)
        turned = jnp.concatenate([dquery[half:], dquery[:half]], axis=0)
        back_q = jnp.zeros((rank_width, REQUEST_ROWS), F32)
        for h in range(group):
            part = slice(h * HD, (h + 1) * HD)
            grad_query = (dquery[:, part] * cos_t + turned[:, part] * sin_t).astype(BF16)
            up_sum[slot, :, part] += scale * contract(uq, grad_query, ((1,), (1,)))
            back_q += contract(bq[:, part], grad_query, ((1,), (0,)))
        up_sum[slot, :, wide:] += scale * contract(uv, grad_value, ((1,), (0,)))
        back_v = contract(bv, grad_value, ((1,), (1,)))
        back = scale * jnp.concatenate([back_q, back_v], axis=0)
        back_out[n] = before[n] + back if has_before else back
    up_out[...] = up_sum[...].astype(BF16)


def attention(scalars, acc, downs, packs, dout, tables, before, j, blocks, group, width, slots):
    rank_width = packs.shape[1]
    wide = group * HD
    query_columns = dout.shape[1]
    query_from = 2 * width + j * wide
    value_from = 2 * width + query_columns + j * HD
    befores = () if before is None else (before,)
    small = (blocks, 2 * rank_width, REQUEST_ROWS)
    up_shape = (slots, rank_width, wide + HD)
    return pl.pallas_call(
        functools.partial(
            attention_kernel, blocks, group, rank_width, query_from, value_from, bool(befores)
        ),
        out_shape=(jax.ShapeDtypeStruct(up_shape, BF16), jax.ShapeDtypeStruct(small, F32)),
        grid_spec=pltpu.PrefetchScalarGridSpec(
            num_scalar_prefetch=1,
            grid=(1,),
            in_specs=[
                whole(acc.shape),
                whole(small),
                whole(small),
                whole(packs.shape),
                pl.BlockSpec((dout.shape[0], wide), lambda i, s: (0, j)),
                *[whole(table.shape) for table in tables],
                *[whole(small) for _ in befores],
            ],
            out_specs=(whole(up_shape), whole(small)),
            scratch_shapes=[pltpu.VMEM(up_shape, F32)],
        ),
        name="attention",
    )(scalars, acc, *downs, packs, dout, *tables, *befores)


def low_kernel(blocks, rank_width, scalars, tokens, back, back_other, out, total):
    total[...] = jnp.zeros_like(total)
    row = lax.broadcasted_iota(jnp.int32, (2 * rank_width, REQUEST_ROWS), 0)
    row = jnp.where(row >= rank_width, row - rank_width, row)
    for n in range(blocks):
        rank = scalar(scalars, 1, n, blocks)
        slot = scalar(scalars, 2, n, blocks)
        kept = ((back[n] + back_other[n]) * (row < rank).astype(F32)).astype(BF16)
        total[slot] += contract(kept, tokens[block_rows(n)], ((1,), (0,)))
    out[...] = total[...].astype(BF16)


def low_products(scalars, tokens, backs, blocks, width, slots):
    small = backs[0].shape
    rank_width = small[1] // 2
    out = (slots, 2 * rank_width, width)
    return pl.pallas_call(
        functools.partial(low_kernel, blocks, rank_width),
        out_shape=jax.ShapeDtypeStruct(out, BF16),
        grid_spec=pltpu.PrefetchScalarGridSpec(
            num_scalar_prefetch=1,
            grid=(1,),
            in_specs=[
                pl.BlockSpec((tokens.shape[0], width), lambda i, s: (0, s[1])),
                whole(small),
                whole(small),
            ],
            out_specs=whole(out),
            scratch_shapes=[pltpu.VMEM(out, F32)],
        ),
        name="low",
    )(scalars, tokens, *backs)


def halves_over(value, axis, send_type):
    count = lax.axis_size(axis)
    step = 1
    pair = (value, jnp.zeros_like(value))
    while step < count:
        value = value if step == 1 else pair[0] + pair[1].astype(F32)
        sent = value.astype(F32 if step == 1 else send_type)
        pairs = [(i, i ^ step) for i in range(count)]
        pair = (value, lax.ppermute(sent, axis, pairs))
        step *= 2
    return pair


def swap_groups(piece, holders, groups, count):
    pairs = [
        (g * count + d, ((g + 1) % groups) * count + d) for g in range(groups) for d in holders
    ]
    return lax.ppermute(piece, ("groups", "dp"), pairs)


def spread_over_tensor(part, holders, tensors):
    parts = [part]
    t = lax.axis_index("tensor")
    step = tensors // 2
    while step:
        pairs = [(d * tensors + i, d * tensors + (i ^ step)) for d in holders for i in range(tensors)]
        mine = jnp.concatenate(parts, axis=1)
        other = lax.ppermute(mine, ("dp", "tensor"), pairs)
        low = (t & step) == 0
        first, second = jnp.where(low, mine, other), jnp.where(low, other, mine)
        cut = part.shape[1]
        parts = [
            side[:, k * cut : (k + 1) * cut] for k in range(len(parts)) for side in (first, second)
        ]
        step //= 2
    return jnp.concatenate(parts, axis=1)


def columns(array, start, size):
    return lax.dynamic_slice_in_dim(array, start, size, 1)


def line_sums(tokens, piece_rows, shard_rows, count_pieces, pack, groups, tensors):
    half = shard_rows // groups
    me, g = lax.axis_index("dp"), lax.axis_index("groups")
    across = [(1, 2), (2, 1)]
    pairs = [(0, 1), (1, 0), (2, 3), (3, 2)]
    outward = [(1, 0), (2, 3)]
    inward = [(0, 1), (3, 2)]
    at_end = (me == 0) | (me == 3)
    upper = me >= 2
    inner = jnp.where(at_end, jnp.where(upper, 2, 1), jnp.where(upper, 1, 2))
    far = jnp.where(upper, 0, 3)
    outer = jnp.where(upper, 3, 0)
    each = range(count_pieces)

    mine = [piece_rows(j, g * half, half) for j in each]
    rest = [piece_rows(j, (1 - g) * half, half) for j in each]
    crossing = [lax.ppermute(mine[j], "dp", across) for j in each]
    paired = [lax.ppermute(mine[j], "dp", pairs) for j in each]
    rests = [lax.ppermute(rest[j], "dp", inward) for j in each]
    inners = [jnp.where(at_end, b, a) for a, b in zip(crossing, paired, strict=True)]
    fars = [lax.ppermute(paired[j], "dp", across) for j in each]
    inner_rests = [swap_groups(inners[j], range(4), groups, 4) for j in each]
    far_rests = [swap_groups(fars[j], (1, 2), groups, 4) for j in each]

    sent = 2 * shard_rows // tensors
    at = lax.axis_index("tensor") * sent
    chunk = jnp.where(upper, 1 - at // shard_rows, 2 + at // shard_rows)
    guest = columns(tokens, chunk * shard_rows + at % shard_rows, sent)
    guest = lax.ppermute(guest, "dp", inward)
    guest = spread_over_tensor(guest, (1, 2), tensors)

    pack_pair = jnp.concatenate([pack, lax.ppermute(pack, "dp", pairs)], axis=0)
    pack_far = lax.ppermute(pack_pair, "dp", across)
    pack_out = lax.ppermute(pack_far, "dp", outward)
    packs = jnp.concatenate([pack_pair, jnp.where(at_end, pack_out, pack_far)], axis=0)

    stacked = []
    for k, owner in enumerate((inner, far)):
        for which in (g, 1 - g):
            own = columns(tokens, owner * shard_rows + which * half, half)
            stacked.append(
                jnp.concatenate([own, columns(guest, k * shard_rows + which * half, half)], axis=0)
            )
    outs = []
    for which in (g, 1 - g):
        own = columns(tokens, outer * shard_rows + which * half, half)
        outs.append(jnp.where(at_end, jnp.zeros_like(own), own))
    owns = [columns(tokens, me * shard_rows + which * half, half) for which in (g, 1 - g)]

    def dot(left, right):
        return jnp.dot(left, right, preferred_element_type=F32)

    rows = tokens.shape[0]
    sums = []
    for j in each:
        total = dot(owns[0], mine[j]) + dot(owns[1], rest[j])
        total = total + dot(outs[0], paired[j]) + dot(outs[1], rests[j])
        both = dot(stacked[0], inners[j]) + dot(stacked[1], inner_rests[j])
        both = both + dot(stacked[2], fars[j]) + dot(stacked[3], far_rests[j])
        given = lax.ppermute(both[rows:].astype(BF16), "dp", outward)
        sums.append(total + both[:rows] + given.astype(F32))
    order = [me, jnp.where(at_end, inner, outer)]
    order += [jnp.where(upper, 1, 2), jnp.where(upper, 0, 3)]
    return sums, packs, order


def takes_line(count, groups, tensors):
    return count == 4 and groups == 2 and tensors & (tensors - 1) == 0


def gradients(
    tokens, w_query, w_key, w_value, a_query, b_query, a_value, b_value,
    adapter_ranks, adapter_slot, block_adapter, live_tokens, d_heads,
):
    blocks = tokens.shape[0] // REQUEST_ROWS
    owned, width, rank_width = a_query.shape
    shard_rows, query_columns = w_query.shape
    value_columns = w_key.shape[1]
    local_kv = value_columns // HD
    group = query_columns // value_columns
    wide = group * HD
    count, groups = lax.axis_size("dp"), lax.axis_size("groups")
    slots = owned * count
    tensors = lax.axis_size("tensor")
    by_line = takes_line(count, groups, tensors) and owned == 1

    block_ids = block_adapter[:, 0]
    slot_ids = adapter_slot[block_ids]
    ranks = adapter_ranks[block_ids]
    pack = jnp.concatenate(
        [jnp.swapaxes(a_query, 1, 2), jnp.swapaxes(a_value, 1, 2), b_query, b_value], axis=2
    )

    def piece_rows(j, start, size):
        return jnp.concatenate(
            [
                lax.dynamic_slice(w_query, (start, j * wide), (size, wide)),
                lax.dynamic_slice(w_key, (start, j * HD), (size, HD)),
                lax.dynamic_slice(w_value, (start, j * HD), (size, HD)),
            ],
            axis=1,
        )

    if by_line:
        sums, packs, order = line_sums(
            tokens, piece_rows, shard_rows, local_kv, pack, groups, tensors
        )
        place = jnp.zeros_like(slot_ids)
        for k, owner in enumerate(order):
            place = jnp.where(slot_ids == owner, k, place)
    else:
        packs = lax.all_gather(pack, "dp", axis=0, tiled=True)
        place = slot_ids
        sums = [
            jnp.dot(
                tokens,
                lax.all_gather(piece_rows(j, 0, shard_rows), "dp", axis=0, tiled=True),
                preferred_element_type=F32,
            )
            for j in range(local_kv)
        ]

    scalars = jnp.concatenate(
        [
            live_tokens[:1],
            lax.axis_index("tensor").astype(jnp.int32)[None],
            place.astype(jnp.int32),
            ranks,
            slot_ids,
        ]
    )
    down = down_products(scalars, tokens, packs, blocks, width)
    downs = halves_over(down, "tensor", F32)
    tables = rope_tables(REQUEST_ROWS, HD)
    ups, back = [], None
    for j in range(local_kv):
        up, back = attention(
            scalars, sums[j], downs, packs, d_heads, tables, back, j, blocks, group, width, slots
        )
        ups.append(up)
    backs = halves_over(back, "tensor", BF16)
    ups = lax.all_to_all(
        jnp.concatenate(ups, axis=2), "dp", split_axis=0, concat_axis=0, tiled=True
    )
    low = low_products(scalars, tokens, backs, blocks, width, slots)
    low = lax.all_to_all(low, "dp", split_axis=0, concat_axis=0, tiled=True)

    def summed(item):
        item = item.astype(F32).reshape((count, owned) + item.shape[1:])
        return jnp.sum(item, axis=0)

    low = summed(low)
    up = summed(ups)
    part = wide + HD
    return (
        jnp.swapaxes(low[:, :rank_width], 1, 2),
        jnp.concatenate([up[:, :, j * part : j * part + wide] for j in range(local_kv)], axis=2),
        jnp.swapaxes(low[:, rank_width:], 1, 2),
        jnp.concatenate([up[:, :, j * part + wide : (j + 1) * part] for j in range(local_kv)], axis=2),
    )


def solution(mesh):
    in_specs = (
        P(("groups", "dp"), None),
        P("dp", "tensor"),
        P("dp", "tensor"),
        P("dp", "tensor"),
        P(("groups", "dp"), "tensor", None),
        P(("groups", "dp"), None, "tensor"),
        P(("groups", "dp"), "tensor", None),
        P(("groups", "dp"), None, "tensor"),
        P("groups"),
        P(),
        P(("groups", "dp"), None),
        P(("groups", "dp")),
        P(("groups", "dp"), "tensor"),
    )
    out_specs = (
        P(("groups", "dp"), "tensor", None),
        P(("groups", "dp"), None, "tensor"),
        P(("groups", "dp"), "tensor", None),
        P(("groups", "dp"), None, "tensor"),
    )
    return jax.shard_map(
        gradients, mesh=mesh, in_specs=in_specs, out_specs=out_specs, check_vma=False
    )
```
